128 devices in a mesh: grp: 4 (over y_lo, core), blk: 32 (over z, x, y_hi).
Axes of the slice: x: 4, y: 4 (y_hi: 2, y_lo: 2; y = y_hi * 2 + y_lo), z: 4, core: 2. Of those that a mesh axis runs over, the one named last changes fastest.
Arguments:
- ratings: bfloat16 [8, 131072, 512], P(None, ('grp', 'blk')), may hold values from -6 to 6
- rated: int32 [8, 131072, 512], P(None, ('grp', 'blk')), may hold values 0 or 1
- user_factors: float32 [131072, 256], P(('grp', 'blk')), may hold values from -1.5 to 1.5
- item_ahead: bfloat16 [32768, 256], P(('grp', 'blk')), may hold values from -1.5 to 1.5
- item_behind: bfloat16 [32768, 256], P(('grp', 'blk')), may hold values from -1.5 to 1.5
- owners: int32 [2, 128], replicated, may hold values from 0 to 127, each once within a row
Outputs:
- user_out: float32 [131072, 256], P(('grp', 'blk'))
- ahead_out: bfloat16 [32768, 256], P(('grp', 'blk'))
- behind_out: bfloat16 [32768, 256], P(('grp', 'blk'))
The draws below stay inside these ranges and needn't reach their ends.
Inputs may be any that keep to these rules, and one draw needn't show every extreme that they name: `owners`: each row is a permutation of 0 .. 127.
All inputs are finite; a program needn't handle non-finite values. No bound on the sum of `rated` on one device may be relied on, other than what follows from the above.
Results may differ from the reference program's by a relative error of at most 0.0086.
Values may be sent and summed in bfloat16 or wider, within the bound.
No kernel may reach another device: no remote copies, remote signals or barrier semaphores. Data moves between devices by JAX's collectives and lax.ppermute only.
A program may use at most 128 MiB of HBM per device.

```python
import jax
import jax.numpy as jnp

RANK = 256
HALF = 256
U_DEV = 1024
STRATA = 8
USERS = 131072
ITEMS_HALF = 32768
N_GRP = 4
N_BLK = 32
DEVICES = 128


def factor_draw(key, salt, rows):
    values = 0.25 * jax.random.normal(jax.random.fold_in(key, salt), (rows, RANK), jnp.float32)
    return jnp.clip(values, -1.5, 1.5)


def draw_user_factors(key, part):
    return factor_draw(key, 101, USERS).astype(jnp.float32)


def draw_item_ahead(key, part):
    return factor_draw(key, 202, ITEMS_HALF).astype(jnp.bfloat16)


def draw_item_behind(key, part):
    return factor_draw(key, 303, ITEMS_HALF).astype(jnp.bfloat16)


def plant(entries, key, low, top_value):
    longest = entries.shape.index(max(entries.shape))
    spots = []
    for shift in (0, 1):
        where = [jax.random.randint(jax.random.fold_in(key, axis), (), 0, length) for axis, length in enumerate(entries.shape)]
        where[longest] = (where[longest] + shift) % entries.shape[longest]
        spots.append(tuple(where))
    return entries.at[spots[0]].set(low).at[spots[1]].set(top_value)


def shard_levels(stream_key, extent, pieces, smallest, top_value):
    def one(dim, parts):
        heights = jax.random.uniform(jax.random.fold_in(jax.random.fold_in(stream_key, 6), dim), (parts,), jnp.float32, smallest / len(pieces), top_value / len(pieces))
        return jnp.repeat(jnp.exp(heights), extent[dim] // parts).reshape((-1,) + (1,) * (len(extent) - dim - 1))

    gain = one(*pieces[0])
    for cut in pieces[1:]:
        gain = gain * one(*cut)
    return gain


def bell_draw(own_key, extent, deviation, bound, split=(), held_as=jnp.bfloat16):
    entries = jax.random.normal(own_key, extent, jnp.float32) * deviation
    if len(split) > 0:
        entries = shard_levels(own_key, extent, split, -0.22, 0.18) * entries
    return jnp.clip(entries, min=-bound, max=bound).astype(held_as)


def setup_inputs(seed: int = 0) -> dict:
    splits = jax.random.split(jax.random.key(seed), 7)
    ratings = bell_draw(splits[0], (STRATA, USERS, 2 * HALF), 1.0, 6.0, ((1, 128),))
    rated = plant((jax.random.randint(splits[1], (STRATA, USERS, 2 * HALF), 0, 2) < 1).astype(jnp.int32), jax.random.fold_in(splits[1], 1), 0, 1)
    user_factors = draw_user_factors(jax.random.fold_in(splits[6], 71), 0)
    item_ahead = draw_item_ahead(jax.random.fold_in(splits[6], 71), 0)
    item_behind = draw_item_behind(jax.random.fold_in(splits[6], 71), 0)
    owners = jax.vmap(lambda own: jax.random.permutation(own, DEVICES))(jax.random.split(splits[5], 2)).reshape((2, DEVICES)).astype(jnp.int32)
    return dict(ratings=ratings, rated=rated, user_factors=user_factors, item_ahead=item_ahead, item_behind=item_behind, owners=owners)


RATE = 0.005
DECAY = 0.05


def reference(ratings, rated, user_factors, item_ahead, item_behind, owners):
    count = N_GRP * N_BLK
    users = user_factors.reshape(count, U_DEV, RANK)
    ahead = item_ahead.reshape(count, HALF, RANK)
    behind = item_behind.reshape(count, HALF, RANK)
    for stratum in range(STRATA):
        if stratum == STRATA // 2:
            ahead = jnp.zeros_like(ahead).at[owners[0]].set(ahead)
            behind = jnp.zeros_like(behind).at[owners[1]].set(behind)
        block = jnp.concatenate([ahead, behind], axis=1)
        block_f = block.astype(jnp.float32)
        user_b = users.astype(jnp.bfloat16).astype(jnp.float32)
        pred = jnp.einsum('nur,nir->nui', user_b, block_f)
        target = ratings[stratum].reshape(count, U_DEV, 2 * HALF).astype(jnp.float32)
        mask = rated[stratum].reshape(count, U_DEV, 2 * HALF)
        err = jnp.where(mask == 1, pred - target, 0.0).astype(jnp.bfloat16).astype(jnp.float32)
        grad_user = jnp.einsum('nui,nir->nur', err, block_f)
        grad_item = jnp.einsum('nui,nur->nir', err, user_b)
        users = users - RATE * (grad_user + DECAY * users)
        block = (block_f - RATE * (grad_item + DECAY * block_f)).astype(jnp.bfloat16)
        ahead = block[:, :HALF]
        behind = block[:, HALF:]
        if stratum < STRATA - 1:
            ahead = jnp.roll(ahead, 1, axis=0)
            behind = jnp.roll(behind, -1, axis=0)
    return (users.reshape(count * U_DEV, RANK),
            ahead.reshape(count * HALF, RANK),
            behind.reshape(count * HALF, RANK))
```

```python
import jax
import jax.numpy as jnp
from jax import lax
from jax.experimental import pallas as pl
from jax.experimental.pallas import tpu as pltpu
from jax.sharding import PartitionSpec as P

RATE = 0.005
DECAY = 0.05
UNRATED = 64.0
AXES = ("grp", "blk")


def code_kernel(rated_ref, ratings_ref, out_ref):
    held = jnp.where(rated_ref[0] == 1, ratings_ref[0].astype(jnp.float32), UNRATED)
    out_ref[...] = held.T.astype(jnp.bfloat16)


def coded(rated, ratings, stratum, tile=256):
    _, users, items = rated.shape
    return pl.pallas_call(
        code_kernel,
        grid=(users // tile,),
        in_specs=[
            pl.BlockSpec((1, tile, items), lambda i: (stratum, i, 0)),
            pl.BlockSpec((1, tile, items), lambda i: (stratum, i, 0)),
        ],
        out_specs=pl.BlockSpec((items, tile), lambda i: (0, i)),
        out_shape=jax.ShapeDtypeStruct((items, users), jnp.bfloat16),
        cost_estimate=pl.CostEstimate(
            flops=users * items, bytes_accessed=users * items * 8, transcendentals=0
        ),
        name=f"code{stratum}",
    )(rated, ratings)


def place_kernel(dest_ref, x_ref, y_ref):
    for j in range(x_ref.shape[0]):
        y_ref[dest_ref[j]] = x_ref[j]


def placed(x, dest):
    return pl.pallas_call(
        place_kernel,
        in_specs=[
            pl.BlockSpec(memory_space=pltpu.SMEM),
            pl.BlockSpec(memory_space=pltpu.VMEM),
        ],
        out_specs=pl.BlockSpec(memory_space=pltpu.VMEM),
        out_shape=jax.ShapeDtypeStruct(x.shape, x.dtype),
        name="place",
    )(dest, x)


def ring(array, by):
    count = lax.axis_size(AXES)
    return lax.ppermute(array, AXES, [(i, (i + by) % count) for i in range(count)])


def all_to_all(x):
    return lax.all_to_all(x, AXES, split_axis=0, concat_axis=0, tiled=True)


def reassigned(ahead, behind, owners):
    half, rank = ahead.shape
    both = jnp.concatenate([ahead, behind], axis=0)
    rows, cols = 2 * half // 8, rank // 128
    tiles = both.reshape(rows, 8, cols, 128).transpose(0, 2, 1, 3).reshape(rows * cols, 8, 128)
    count = rows * cols
    spread = all_to_all(tiles)
    after = jnp.roll(owners[0], -1)
    before = jnp.roll(owners[1], 1)
    dest = jnp.where(lax.axis_index(AXES) < count // 2, after, before)
    got = all_to_all(placed(spread, dest))
    both = got.reshape(rows, cols, 8, 128).transpose(0, 2, 1, 3).reshape(2 * half, rank)
    return both[:half], both[half:]


def errors(code, block, user_b):
    pred = lax.dot_general(
        block, user_b, (((1,), (1,)), ((), ())), preferred_element_type=jnp.float32
    )
    value = code.astype(jnp.float32)
    return jnp.where(value < UNRATED, pred - value, 0.0).astype(jnp.bfloat16)


def updated(block, err, user_b):
    grad = jnp.dot(err, user_b, preferred_element_type=jnp.float32)
    held = block.astype(jnp.float32)
    return (held - RATE * (grad + DECAY * held)).astype(jnp.bfloat16)


def back(err, block):
    return lax.dot_general(
        err, block, (((0,), (0,)), ((), ())), preferred_element_type=jnp.float32
    )


def body(ratings, rated, user_factors, item_ahead, item_behind, owners):
    half = item_ahead.shape[0]
    users, ahead, behind = user_factors, item_ahead, item_behind
    strata = ratings.shape[0]
    for s in range(strata):
        code = coded(rated, ratings, s)
        user_b = users.astype(jnp.bfloat16)
        err_a = errors(code[:half], ahead, user_b)
        new_a = updated(ahead, err_a, user_b)
        err_b = errors(code[half:], behind, user_b)
        new_b = updated(behind, err_b, user_b)
        grad = back(err_a, ahead) + back(err_b, behind)
        users = users - RATE * (grad + DECAY * users)
        ahead, behind = new_a, new_b
        if s == strata // 2 - 1:
            ahead, behind = reassigned(ahead, behind, owners)
        elif s < strata - 1:
            ahead, behind = ring(ahead, 1), ring(behind, -1)
    return users, ahead, behind


def solution(mesh):
    rows = P(AXES, None)
    in_specs = (P(None, AXES, None), P(None, AXES, None), rows, rows, rows, P())
    return jax.shard_map(
        body, mesh=mesh, in_specs=in_specs, out_specs=(rows, rows, rows), check_vma=False
    )
```

```python
import functools

import jax
import jax.numpy as jnp
from jax import lax
from jax.experimental import pallas as pl
from jax.experimental.pallas import tpu as pltpu
from jax.sharding import PartitionSpec as P


RATE = 0.005
DECAY = 0.05
UNRATED = 64.0
AXES = ("grp", "blk")


ANY = pl.BlockSpec(memory_space=pl.ANY)
FAST = pl.BlockSpec(memory_space=pltpu.VMEM)


def marked(rated, ratings):
    return jnp.where(rated == 1, ratings.astype(jnp.float32), UNRATED).astype(jnp.bfloat16)


def own_parity():
    return lax.axis_index("blk") & 1


def code_kernel(start, rated, ratings, token, out, rated_buf, ratings_buf, sems):
    slots, tile, items = rated_buf.shape
    half, parts = items // 2, out.shape[2] // tile

    def fetches(slot, stratum, part):
        rows = pl.ds(pl.multiple_of(part * tile, tile), tile)
        return (
            pltpu.make_async_copy(rated.at[stratum, rows], rated_buf.at[slot], sems.at[0, slot]),
            pltpu.make_async_copy(ratings.at[stratum, rows], ratings_buf.at[slot], sems.at[1, slot]),
        )

    for slot in range(slots):
        for fetch in fetches(slot, start + slot // parts, slot % parts):
            fetch.start()
    parity = own_parity()

    def code(slot, carry):
        t, part = slot // parts, lax.rem(slot, parts)
        for fetch in fetches(slot, start + t, part):
            fetch.wait()
        held = marked(rated_buf[slot], ratings_buf[slot])
        rows = pl.ds(pl.multiple_of(part * tile, tile), tile)
        out[t, parity, rows, :] = held[:, :half]
        out[t, 1 - parity, rows, :] = held[:, half:]
        return carry

    lax.fori_loop(0, slots, code, 0)


def coded(rated, ratings, start, stop, token, tile=256):
    _, users, items = rated.shape
    count = stop - start
    slots = count * (users // tile)
    return pl.pallas_call(
        functools.partial(code_kernel, start),
        in_specs=[ANY, ANY, ANY],
        out_specs=FAST,
        out_shape=jax.ShapeDtypeStruct((count, 2, users, items // 2), jnp.bfloat16),
        scratch_shapes=[
            pltpu.VMEM((slots, tile, items), jnp.int32),
            pltpu.VMEM((slots, tile, items), jnp.bfloat16),
            pltpu.SemaphoreType.DMA((2, slots)),
        ],
        compiler_params=pltpu.CompilerParams(vmem_limit_bytes=(count * 4 + 2) << 20),
        cost_estimate=pl.CostEstimate(
            flops=count * users * items,
            bytes_accessed=count * users * items * 8,
            transcendentals=0,
        ),
    )(rated, ratings, token)


def half_kernel(plane, tile, rated, ratings, token, out, rated_buf, ratings_buf, sems):
    half = out.shape[1]
    cols = pl.ds(pl.multiple_of((own_parity() ^ plane) * half, half), half)
    coming = []
    for i in range(out.shape[0] // tile):
        rows = pl.ds(i * tile, tile)
        pair = (
            pltpu.make_async_copy(rated.at[0, rows, cols], rated_buf.at[rows], sems.at[0, i]),
            pltpu.make_async_copy(ratings.at[0, rows, cols], ratings_buf.at[rows], sems.at[1, i]),
        )
        for fetch in pair:
            fetch.start()
        coming.append((rows, pair))
    for rows, pair in coming:
        for fetch in pair:
            fetch.wait()
        out[rows, :] = marked(rated_buf[rows, :], ratings_buf[rows, :])


def first_kernel(plane, tile, rated, ratings, users_in, ahead, behind, out, users, user_b, blocks,
                 rated_buf, ratings_buf, sems, more_sems):
    parity = own_parity()
    others = (
        pltpu.make_async_copy(users_in, users, more_sems.at[0]),
        pltpu.make_async_copy(ahead, blocks.at[parity], more_sems.at[1]),
        pltpu.make_async_copy(behind, blocks.at[1 - parity], more_sems.at[2]),
    )
    for other in others:
        other.start()
    half_kernel(plane, tile, rated, ratings, None, out, rated_buf, ratings_buf, sems)
    for other in others:
        other.wait()
    user_b[...] = users[...].astype(jnp.bfloat16)


def half_scratch(users, half, tile):
    return [
        pltpu.VMEM((users, half), jnp.int32),
        pltpu.VMEM((users, half), jnp.bfloat16),
        pltpu.SemaphoreType.DMA((2, users // tile)),
    ]


def opened(rated, ratings, users, ahead, behind, plane, tile=256):
    count, rank = users.shape
    half = ahead.shape[0]
    return pl.pallas_call(
        functools.partial(first_kernel, plane, tile),
        in_specs=[ANY] * 5,
        out_specs=[FAST] * 4,
        out_shape=[
            jax.ShapeDtypeStruct((count, half), jnp.bfloat16),
            jax.ShapeDtypeStruct((count, rank), jnp.float32),
            jax.ShapeDtypeStruct((count, rank), jnp.bfloat16),
            jax.ShapeDtypeStruct((2, half, rank), jnp.bfloat16),
        ],
        scratch_shapes=half_scratch(count, half, tile) + [pltpu.SemaphoreType.DMA((3,))],
        compiler_params=pltpu.CompilerParams(vmem_limit_bytes=8 << 20),
        name="opened",
    )(rated, ratings, users, ahead, behind)


def coded_half(rated, ratings, plane, token, tile=256):
    _, users, items = rated.shape
    half = items // 2
    return pl.pallas_call(
        functools.partial(half_kernel, plane, tile),
        in_specs=[ANY] * 3,
        out_specs=FAST,
        out_shape=jax.ShapeDtypeStruct((users, half), jnp.bfloat16),
        scratch_shapes=half_scratch(users, half, tile),
        compiler_params=pltpu.CompilerParams(vmem_limit_bytes=4 << 20),
        cost_estimate=pl.CostEstimate(
            flops=users * half, bytes_accessed=users * half * 8, transcendentals=0
        ),
        name="rest",
    )(rated, ratings, token)


def place_kernel(owners, x, y):
    count = x.shape[0]
    me = lax.axis_index("grp") * lax.axis_size("blk") + lax.axis_index("blk")
    row = jnp.where(me < count // 2, 0, 1)
    step = jnp.where(me < count // 2, 1, count - 1)
    for j in range(count):
        y[owners[row, lax.rem(j + step, count)]] = x[j]


def placed(x, owners):
    return pl.pallas_call(
        place_kernel,
        in_specs=[pl.BlockSpec(memory_space=pltpu.SMEM), FAST],
        out_specs=FAST,
        out_shape=jax.ShapeDtypeStruct(x.shape, x.dtype),
        compiler_params=pltpu.CompilerParams(vmem_limit_bytes=2 << 20),
        name="place",
    )(owners, x)


def over_even(array):
    count = lax.axis_size(AXES)
    return lax.ppermute(array, AXES, [(i, i ^ 1) for i in range(count)])


def over_odd(array):
    count = lax.axis_size(AXES)
    pairs = [(i, (i + 1 if i % 2 else i - 1) % count) for i in range(count)]
    return lax.ppermute(array, AXES, pairs)


MOVES = (over_even, over_odd)
FIRST = (1, 0, 1, 0)
CODED = {0: (1, 4), 3: (4, 5), 4: (5, 8)}


def all_to_all(x):
    return lax.all_to_all(x, AXES, split_axis=0, concat_axis=0, tiled=True)


def reassigned(ahead, behind, owners):
    half, rank = ahead.shape
    both = jnp.concatenate([ahead, behind], axis=0)
    rows, cols = 2 * half // 8, rank // 128
    tiles = both.reshape(rows, 8, cols, 128).transpose(0, 2, 1, 3).reshape(rows * cols, 8, 128)
    spread = all_to_all(tiles)
    sorted_tiles = placed(spread, owners)
    got = all_to_all(sorted_tiles)
    both = got.reshape(rows, cols, 8, 128).transpose(0, 2, 1, 3).reshape(2 * half, rank)
    return both[:half], both[half:]


def errors(code, block, user_b):
    pred = lax.dot_general(
        user_b, block, (((1,), (1,)), ((), ())), preferred_element_type=jnp.float32
    )
    value = code.astype(jnp.float32)
    return jnp.where(value < UNRATED, pred - value, 0.0).astype(jnp.bfloat16)


def updated(block, err, user_b):
    grad = lax.dot_general(
        err, user_b, (((0,), (0,)), ((), ())), preferred_element_type=jnp.float32
    )
    held = block.astype(jnp.float32)
    return (held - RATE * (grad + DECAY * held)).astype(jnp.bfloat16)


def back(err, block):
    return jnp.dot(err, block, preferred_element_type=jnp.float32)


def body(ratings, rated, user_factors, item_ahead, item_behind, owners):
    def held(x):
        return pltpu.with_memory_space_constraint(x, pltpu.HBM)

    rated, ratings = held(rated), held(ratings)
    strata = ratings.shape[0]
    middle = strata // 2
    even, item_ahead = lax.optimization_barrier((own_parity() == 0, item_ahead))

    def swapped(a, b):
        return jnp.where(even, a, b), jnp.where(even, b, a)

    code, users, user_b, blocks = opened(
        rated, ratings, held(user_factors), held(item_ahead), held(item_behind), FIRST[0]
    )
    codes = [None] * strata
    codes[0] = [code, code]
    for s in range(strata):
        first = FIRST[s % 4]
        second = 1 - first
        stays = s in (middle - 1, strata - 1)
        errs, moved, came = [None, None], [None, None], [None, None]
        if s > 0:
            user_b = users.astype(jnp.bfloat16)
        errs[first] = errors(codes[s][first], blocks[first], user_b)
        moved[first] = updated(blocks[first], errs[first], user_b)
        if not stays:
            came[second] = MOVES[first](moved[first])
        moved[first], user_c = lax.optimization_barrier((moved[first], user_b))
        if s == 0:
            codes[0][second] = coded_half(rated, ratings, second, moved[first])
        errs[second] = errors(codes[s][second], blocks[second], user_c)
        moved[second] = updated(blocks[second], errs[second], user_c)
        if not stays:
            came[first] = MOVES[second](moved[second])
        if s in CODED:
            start, stop = CODED[s]
            codes[start:stop] = coded(rated, ratings, start, stop, moved[second])
        grad = back(errs[0], blocks[0]) + back(errs[1], blocks[1])
        users = users - RATE * (grad + DECAY * users)
        if s == middle - 1:
            came = swapped(*reassigned(*swapped(*moved), owners))
        blocks = came
    ahead, behind = swapped(*moved)
    return users, ahead, behind


def solution(mesh):
    rows = P(AXES, None)
    in_specs = (P(None, AXES, None), P(None, AXES, None), rows, rows, rows, P())
    return jax.shard_map(
        body, mesh=mesh, in_specs=in_specs, out_specs=(rows, rows, rows), check_vma=False
    )
```

```python
import functools

import jax
import jax.numpy as jnp
from jax import lax
from jax.experimental import pallas as pl
from jax.experimental.pallas import tpu as pltpu
from jax.sharding import PartitionSpec as P


RATE = 0.005
DECAY = 0.05
UNRATED = 64.0
AXES = ("grp", "blk")


ANY = pl.BlockSpec(memory_space=pl.ANY)
FAST = pl.BlockSpec(memory_space=pltpu.VMEM)


def marked(rated, ratings):
    return jnp.where(rated == 1, ratings.astype(jnp.float32), UNRATED).astype(jnp.bfloat16)


def own_parity():
    return lax.axis_index("blk") & 1


def code_kernel(start, rated, ratings, token, out, rated_buf, ratings_buf, sems):
    slots, tile, items = rated_buf.shape
    half, parts = items // 2, out.shape[2] // tile

    def fetches(slot, stratum, part):
        rows = pl.ds(pl.multiple_of(part * tile, tile), tile)
        return (
            pltpu.make_async_copy(rated.at[stratum, rows], rated_buf.at[slot], sems.at[0, slot]),
            pltpu.make_async_copy(ratings.at[stratum, rows], ratings_buf.at[slot], sems.at[1, slot]),
        )

    for slot in range(slots):
        for fetch in fetches(slot, start + slot // parts, slot % parts):
            fetch.start()
    parity = own_parity()

    def code(slot, carry):
        t, part = slot // parts, lax.rem(slot, parts)
        for fetch in fetches(slot, start + t, part):
            fetch.wait()
        held = marked(rated_buf[slot], ratings_buf[slot])
        rows = pl.ds(pl.multiple_of(part * tile, tile), tile)
        out[t, parity, rows, :] = held[:, :half]
        out[t, 1 - parity, rows, :] = held[:, half:]
        return carry

    lax.fori_loop(0, slots, code, 0)


def coded(rated, ratings, start, stop, token, tile=256):
    _, users, items = rated.shape
    count = stop - start
    slots = count * (users // tile)
    return pl.pallas_call(
        functools.partial(code_kernel, start),
        in_specs=[ANY, ANY, ANY],
        out_specs=FAST,
        out_shape=pltpu.VMEM(
            (count, 2, users, items // 2), jnp.bfloat16
        ),
        scratch_shapes=[
            pltpu.VMEM((slots, tile, items), jnp.int32),
            pltpu.VMEM((slots, tile, items), jnp.bfloat16),
            pltpu.SemaphoreType.DMA((2, slots)),
        ],
        compiler_params=pltpu.CompilerParams(vmem_limit_bytes=(count * 4 + 2) << 20),
        cost_estimate=pl.CostEstimate(
            flops=count * users * items,
            bytes_accessed=count * users * items * 8,
            transcendentals=0,
        ),
    )(rated, ratings, token)


def half_kernel(plane, tile, rated, ratings, token, out, rated_buf, ratings_buf, sems):
    half = out.shape[1]
    cols = pl.ds(pl.multiple_of((own_parity() ^ plane) * half, half), half)
    coming = []
    for i in range(out.shape[0] // tile):
        rows = pl.ds(i * tile, tile)
        pair = (
            pltpu.make_async_copy(rated.at[0, rows, cols], rated_buf.at[rows], sems.at[0, i]),
            pltpu.make_async_copy(ratings.at[0, rows, cols], ratings_buf.at[rows], sems.at[1, i]),
        )
        for fetch in pair:
            fetch.start()
        coming.append((rows, pair))
    for rows, pair in coming:
        for fetch in pair:
            fetch.wait()
        out[rows, :] = marked(rated_buf[rows, :], ratings_buf[rows, :])


def first_kernel(plane, tile, rated, ratings, users_in, ahead, behind, out, users, user_b, blocks,
                 rated_buf, ratings_buf, sems, more_sems):
    parity = own_parity()
    others = (
        pltpu.make_async_copy(users_in, users, more_sems.at[0]),
        pltpu.make_async_copy(ahead, blocks.at[parity], more_sems.at[1]),
        pltpu.make_async_copy(behind, blocks.at[1 - parity], more_sems.at[2]),
    )
    for other in others:
        other.start()
    half_kernel(plane, tile, rated, ratings, None, out, rated_buf, ratings_buf, sems)
    for other in others:
        other.wait()
    user_b[...] = users[...].astype(jnp.bfloat16)


def half_scratch(users, half, tile):
    return [
        pltpu.VMEM((users, half), jnp.int32),
        pltpu.VMEM((users, half), jnp.bfloat16),
        pltpu.SemaphoreType.DMA((2, users // tile)),
    ]


def opened(rated, ratings, users, ahead, behind, plane, tile=256):
    count, rank = users.shape
    half = ahead.shape[0]
    return pl.pallas_call(
        functools.partial(first_kernel, plane, tile),
        in_specs=[ANY] * 5,
        out_specs=[FAST] * 4,
        out_shape=[
            jax.ShapeDtypeStruct((count, half), jnp.bfloat16),
            jax.ShapeDtypeStruct((count, rank), jnp.float32),
            jax.ShapeDtypeStruct((count, rank), jnp.bfloat16),
            jax.ShapeDtypeStruct((2, half, rank), jnp.bfloat16),
        ],
        scratch_shapes=half_scratch(count, half, tile) + [pltpu.SemaphoreType.DMA((3,))],
        compiler_params=pltpu.CompilerParams(vmem_limit_bytes=8 << 20),
        name="opened",
    )(rated, ratings, users, ahead, behind)


def coded_half(rated, ratings, plane, token, tile=256):
    _, users, items = rated.shape
    half = items // 2
    return pl.pallas_call(
        functools.partial(half_kernel, plane, tile),
        in_specs=[ANY] * 3,
        out_specs=FAST,
        out_shape=jax.ShapeDtypeStruct((users, half), jnp.bfloat16),
        scratch_shapes=half_scratch(users, half, tile),
        compiler_params=pltpu.CompilerParams(vmem_limit_bytes=4 << 20),
        cost_estimate=pl.CostEstimate(
            flops=users * half, bytes_accessed=users * half * 8, transcendentals=0
        ),
        name="rest",
    )(rated, ratings, token)


def close_kernel(t, plane, tile, code, block, moved, grad, user_b, users, users_out, ahead_out,
                 behind_out, err, users_buf, new, sems):
    parity = own_parity()

    def send(source, plane, sem):
        @pl.when(parity == plane)
        def _():
            pltpu.make_async_copy(source, ahead_out, sem).start()

        @pl.when(parity != plane)
        def _():
            pltpu.make_async_copy(source, behind_out, sem).start()

    send(moved, 1 - plane, sems.at[0])
    held = block[...]
    parts = user_b.shape[0] // tile
    going = []
    for i in range(parts):
        rows = pl.ds(i * tile, tile)
        pred = lax.dot_general(
            user_b[rows, :], held, (((1,), (1,)), ((), ())), preferred_element_type=jnp.float32
        )
        value = code[t, plane, rows, :].astype(jnp.float32)
        err[rows, :] = jnp.where(value < UNRATED, pred - value, 0.0).astype(jnp.bfloat16)
        more = jnp.dot(err[rows, :], held, preferred_element_type=jnp.float32)
        old = users[rows, :]
        users_buf[rows, :] = old - RATE * (grad[rows, :] + more + DECAY * old)
        going.append(pltpu.make_async_copy(users_buf.at[rows], users_out.at[rows], sems.at[2 + i]))
        going[-1].start()
    more = lax.dot_general(
        err[...], user_b[...], (((0,), (0,)), ((), ())), preferred_element_type=jnp.float32
    )
    held = held.astype(jnp.float32)
    new[...] = (held - RATE * (more + DECAY * held)).astype(jnp.bfloat16)
    send(new, plane, sems.at[1])
    for copy in going:
        copy.wait()
    pltpu.make_async_copy(moved, ahead_out, sems.at[0]).wait()
    pltpu.make_async_copy(new, behind_out, sems.at[1]).wait()


def closed(code, block, moved, grad, user_b, users, tile=256):
    codes, t, plane = code
    count, rank = users.shape
    return pl.pallas_call(
        functools.partial(close_kernel, t, plane, tile),
        in_specs=[FAST] * 6,
        out_specs=[ANY] * 3,
        out_shape=[
            jax.ShapeDtypeStruct(users.shape, users.dtype),
            jax.ShapeDtypeStruct(block.shape, block.dtype),
            jax.ShapeDtypeStruct(block.shape, block.dtype),
        ],
        scratch_shapes=[
            pltpu.VMEM((count, block.shape[0]), jnp.bfloat16),
            pltpu.VMEM((count, rank), jnp.float32),
            pltpu.VMEM(block.shape, block.dtype),
            pltpu.SemaphoreType.DMA((2 + count // tile,)),
        ],
        compiler_params=pltpu.CompilerParams(vmem_limit_bytes=6 << 20),
        name="closed",
    )(codes, block, moved, grad, user_b, users)


def narrow_kernel(users, user_b):
    user_b[...] = users[...].astype(jnp.bfloat16)


def narrowed(users):
    return pl.pallas_call(
        narrow_kernel,
        in_specs=[FAST],
        out_specs=FAST,
        out_shape=pltpu.VMEM(users.shape, jnp.bfloat16),
        compiler_params=pltpu.CompilerParams(vmem_limit_bytes=2 << 20),
        name="narrow",
    )(users)


def part_kernel(t, plane, tile, code, block, user_b, err, new):
    held = block[...]
    for i in range(user_b.shape[0] // tile):
        rows = pl.ds(i * tile, tile)
        pred = lax.dot_general(
            user_b[rows, :], held, (((1,), (1,)), ((), ())), preferred_element_type=jnp.float32
        )
        value = code[t, plane, rows, :].astype(jnp.float32)
        err[rows, :] = jnp.where(value < UNRATED, pred - value, 0.0).astype(jnp.bfloat16)
    grad = lax.dot_general(
        err[...], user_b[...], (((0,), (0,)), ((), ())), preferred_element_type=jnp.float32
    )
    held = held.astype(jnp.float32)
    new[...] = (held - RATE * (grad + DECAY * held)).astype(jnp.bfloat16)


def part(code, block, user_b, tile=256):
    codes, t, plane = code
    users, half = user_b.shape[0], block.shape[0]
    return pl.pallas_call(
        functools.partial(part_kernel, t, plane, tile),
        in_specs=[FAST] * 3,
        out_specs=[FAST] * 2,
        out_shape=[
            jax.ShapeDtypeStruct((users, half), jnp.bfloat16),
            jax.ShapeDtypeStruct(block.shape, jnp.bfloat16),
        ],
        compiler_params=pltpu.CompilerParams(vmem_limit_bytes=4 << 20),
        cost_estimate=pl.CostEstimate(
            flops=4 * users * half * block.shape[1],
            bytes_accessed=2 * users * (half * 3 + block.shape[1]),
            transcendentals=0,
        ),
        name="part",
    )(codes, block, user_b)


def place_kernel(owners, x, y):
    count = x.shape[0]
    me = lax.axis_index("grp") * lax.axis_size("blk") + lax.axis_index("blk")
    row = jnp.where(me < count // 2, 0, 1)
    step = jnp.where(me < count // 2, 1, count - 1)
    for j in range(count):
        y[owners[row, lax.rem(j + step, count)]] = x[j]


def placed(x, owners):
    return pl.pallas_call(
        place_kernel,
        in_specs=[pl.BlockSpec(memory_space=pltpu.SMEM), FAST],
        out_specs=FAST,
        out_shape=jax.ShapeDtypeStruct(x.shape, x.dtype),
        compiler_params=pltpu.CompilerParams(vmem_limit_bytes=2 << 20),
        name="place",
    )(owners, x)


def over_even(array):
    count = lax.axis_size(AXES)
    return lax.ppermute(array, AXES, [(i, i ^ 1) for i in range(count)])


def over_odd(array):
    count = lax.axis_size(AXES)
    pairs = [(i, (i + 1 if i % 2 else i - 1) % count) for i in range(count)]
    return lax.ppermute(array, AXES, pairs)


MOVES = (over_even, over_odd)
FIRST = (1, 0, 1, 0, 1, 0, 1, 1)
CODED = {0: ((1, 4),), 3: ((4, 5),), 4: ((5, 8),)}


def all_to_all(x):
    return lax.all_to_all(x, AXES, split_axis=0, concat_axis=0, tiled=True)


def reassigned(ahead, behind, owners):
    half, rank = ahead.shape
    both = jnp.concatenate([ahead, behind], axis=0)
    rows, cols = 2 * half // 8, rank // 128
    tiles = both.reshape(rows, 8, cols, 128).transpose(0, 2, 1, 3).reshape(rows * cols, 8, 128)
    spread = all_to_all(tiles)
    sorted_tiles = placed(spread, owners)
    got = all_to_all(sorted_tiles)
    both = got.reshape(rows, cols, 8, 128).transpose(0, 2, 1, 3).reshape(2 * half, rank)
    return both[:half], both[half:]


def back(err, block):
    return jnp.dot(err, block, preferred_element_type=jnp.float32)


def body(ratings, rated, user_factors, item_ahead, item_behind, owners):
    def held(x):
        return pltpu.with_memory_space_constraint(x, pltpu.HBM)

    rated, ratings = held(rated), held(ratings)
    strata = ratings.shape[0]
    middle = strata // 2
    even, item_ahead = lax.optimization_barrier((own_parity() == 0, item_ahead))

    def swapped(a, b):
        return jnp.where(even, a, b), jnp.where(even, b, a)

    code, users, user_b, blocks = opened(
        rated, ratings, held(user_factors), held(item_ahead), held(item_behind), FIRST[0]
    )
    codes = [None] * strata
    codes[0] = [(code[None, None], 0, 0)] * 2
    for s in range(strata):
        first = FIRST[s]
        second = 1 - first
        stays = s in (middle - 1, strata - 1)
        errs, moved, came = [None, None], [None, None], [None, None]
        if s not in (0, middle):
            user_b = users.astype(jnp.bfloat16)
        errs[first], moved[first] = part(codes[s][first], blocks[first], user_b)
        if not stays:
            came[second] = MOVES[first](moved[first])
        if s == strata - 1:
            grad = back(errs[first], blocks[first])
            return closed(codes[s][second], blocks[second], moved[first], grad, user_b, users)
        moved[first], user_c = lax.optimization_barrier((moved[first], user_b))
        if s == 0:
            rest = coded_half(rated, ratings, second, moved[first])
            codes[0][second] = (rest[None, None], 0, 0)
        errs[second], moved[second] = part(codes[s][second], blocks[second], user_c)
        if not stays:
            came[first] = MOVES[second](moved[second])
        for start, stop in CODED.get(s, ()):
            held = coded(rated, ratings, start, stop, moved[second])
            codes[start:stop] = [[(held, t, k) for k in (0, 1)] for t in range(stop - start)]
        grad = back(errs[0], blocks[0]) + back(errs[1], blocks[1])
        users = users - RATE * (grad + DECAY * users)
        if s == middle - 1:
            user_b = narrowed(users)
            came = swapped(*reassigned(*swapped(*moved), owners))
        blocks = came


def solution(mesh):
    rows = P(AXES, None)
    in_specs = (P(None, AXES, None), P(None, AXES, None), rows, rows, rows, P())
    return jax.shard_map(
        body, mesh=mesh, in_specs=in_specs, out_specs=(rows, rows, rows), check_vma=False
    )
```
